512 devices in a mesh: dp: 16 (over z_lo, x), seq: 32 (over z_hi, y, core).
Axes of the slice: x: 4, y: 8, z: 8 (z_hi: 2, z_lo: 4; z = z_hi * 4 + z_lo), core: 2. Of those that a mesh axis runs over, the one named last changes fastest.
Arguments:
- qkv: bfloat16 [3, 16, 2, 2048, 4096], P(None, 'dp', None, 'seq'), may hold values from -4 to 4
- master: float32 [4, 4096], P(None, 'dp'), may hold values from -0.9 to 5.2
- moment_one: float32 [4, 4096], P(None, 'dp'), may hold values from -3 to 3
- moment_two: float32 [4, 4096], P(None, 'dp'), may hold values from 0.25 to 4
- grads: float32 [4, 4096], P(None, 'dp'), may hold values from -8 to 8
Outputs:
- attended: bfloat16 [16, 2, 2048, 4096], P('dp', None, 'seq')
- updated: float32 [4, 4096], P(None, 'dp')
- first_moment: float32 [4, 4096], P(None, 'dp')
- second_moment: float32 [4, 4096], P(None, 'dp')
The draws below stay inside these ranges and needn't reach their ends.
All inputs are finite; a program needn't handle non-finite values.
Results may differ from the reference program's by a relative error of at most 0.0011.
The reference program's roundings to bfloat16 on the way count: a program that leaves them out, or rounds other values in their place, can miss the bound.
Values may be sent and summed in bfloat16 or wider, within the bound.
A program may use at most 64 MiB of HBM per device.

```python
import math
import jax
import jax.numpy as jnp
from jax import lax

D = 4096
HEADS = 32
HD = 128
SEQS = 2
OPT_STEP = 10
PATCHES = 2048
N_DP = 16


def draw_qkv(key, part):
    key_one = jax.random.fold_in(key, 11)
    result = jax.random.normal(key_one, (3, N_DP, SEQS, PATCHES, D), jnp.float32)
    return jnp.clip(result, -4.0, 4.0).astype(jnp.bfloat16)


def draw_master(key, part):
    key_two = jax.random.fold_in(key, 22)
    key_three = jax.random.fold_in(key, 23)
    gains = jax.random.uniform(key_two, (2, D), jnp.float32, 0.7, 1.4)
    biases = jnp.clip(0.3 * jax.random.normal(key_three, (2, D), jnp.float32), -0.9, 0.9)
    return jnp.stack([gains[0], biases[0], gains[1], biases[1]]).astype(jnp.float32)


def block_scale(own_key, extent, pieces, low, high):
    loudness, own = 1.0, jax.random.fold_in(own_key, 6)
    for position, shards_of in pieces:
        heights = jnp.exp(jax.random.uniform(jax.random.fold_in(own, position), (shards_of,), jnp.float32, low / len(pieces), high / len(pieces)))
        loudness = loudness * jnp.repeat(heights, extent[position] // shards_of).reshape([-1 if axis == position else 1 for axis in range(len(extent))])
    return loudness


def scatter_about(own_key, shape, scale, limit, cuts=(), kind=jnp.bfloat16):
    values = scale * jax.random.normal(own_key, shape, jnp.float32)
    if cuts:
        values = values * block_scale(own_key, shape, cuts, -0.22, 0.18)
    return jnp.clip(values, -limit, limit).astype(kind)


def setup_inputs(seed: int = 0) -> dict:
    key_of = jax.random.split(jax.random.key(seed), 6)
    qkv = draw_qkv(jax.random.fold_in(key_of[5], 71), 0)
    master = draw_master(jax.random.fold_in(key_of[5], 71), 0)
    moment_one = scatter_about(key_of[2], (4, D), 0.5, 3.0, ((1, 16),), jnp.float32)
    moment_two = jnp.clip(jnp.exp(math.log(4.0) - 2.7725887 * jax.random.uniform(key_of[3], (4, D), jnp.float32) ** block_scale(key_of[3], (4, D), ((1, 16),), -0.2, 0.2)), 0.25, 4.0)
    grads = scatter_about(key_of[4], (4, D), 2.0, 8.0, ((1, 16),), jnp.float32)
    return dict(qkv=qkv, master=master, moment_one=moment_one, moment_two=moment_two, grads=grads)


BETA_ONE = 0.9
BETA_TWO = 0.95
RATE = 0.02
DECAY = 0.1
EPSILON = 1e-08

def adamw(master, moment_one, moment_two, grads):
    first_moment = BETA_ONE * moment_one + (1.0 - BETA_ONE) * grads
    second_moment = BETA_TWO * moment_two + (1.0 - BETA_TWO) * grads * grads
    first_hat = first_moment / (1.0 - BETA_ONE ** OPT_STEP)
    second_hat = second_moment / (1.0 - BETA_TWO ** OPT_STEP)
    updated = master - RATE * (first_hat / (jnp.sqrt(second_hat) + EPSILON) + DECAY * master)
    return (updated, first_moment, second_moment)

def normalize(values, gain_row, bias_row):
    row_count = values.shape[0]
    head_count = values.shape[1] // HD
    grouped = values.astype(jnp.float32).reshape(row_count, head_count, HD)
    centre = lax.optimization_barrier(jnp.mean(grouped, axis=-1, keepdims=True))
    spread = lax.optimization_barrier(jnp.mean((grouped - centre) ** 2, axis=-1, keepdims=True))
    scaled = (grouped - centre) / jnp.sqrt(spread + 1e-06)
    scaled = scaled * gain_row.reshape(head_count, HD) + bias_row.reshape(head_count, HD)
    return scaled.reshape(row_count, head_count * HD).astype(jnp.bfloat16)

def reference(qkv, master, moment_one, moment_two, grads):
    updated, first_moment, second_moment = adamw(master, moment_one, moment_two, grads)
    layer_bf = updated.astype(jnp.bfloat16)
    layer_bf = lax.optimization_barrier(layer_bf)
    layer_full = layer_bf.astype(jnp.float32)
    sample_count = N_DP * SEQS
    samples = qkv.reshape(3, sample_count, PATCHES, D)
    scale_value = HD ** (-0.5)

    def one_sample(sample_id):
        span_rows = lax.dynamic_index_in_dim(samples, sample_id, 1, keepdims=False)
        queries = normalize(span_rows[0], layer_full[0], layer_full[1])
        key_rows = normalize(span_rows[1], layer_full[2], layer_full[3])
        query_heads = queries.reshape(PATCHES, HEADS, HD).transpose(1, 0, 2)
        key_heads = key_rows.reshape(PATCHES, HEADS, HD).transpose(1, 0, 2)
        value_heads = span_rows[2].reshape(PATCHES, HEADS, HD).transpose(1, 0, 2)

        def one_head(triple):
            query_one, key_one, value_one = triple
            scores = jnp.dot(query_one, key_one.T, preferred_element_type=jnp.float32) * scale_value
            probs = jax.nn.softmax(scores, axis=-1).astype(jnp.bfloat16)
            return jnp.dot(probs, value_one, preferred_element_type=jnp.float32).astype(jnp.bfloat16)
        head_outs = lax.map(one_head, (query_heads, key_heads, value_heads))
        return head_outs.transpose(1, 0, 2).reshape(PATCHES, HEADS * HD)
    outputs = lax.map(one_sample, jnp.arange(sample_count, dtype=jnp.int32))
    attended = outputs.reshape(N_DP, SEQS, PATCHES, D)
    return (attended, updated, first_moment, second_moment)
```

```python
import functools

import jax
import jax.numpy as jnp
from jax import lax
from jax.experimental import pallas as pl
from jax.experimental.pallas import tpu as pltpu
from jax.sharding import PartitionSpec as P

HEADS = 32
HD = 128
OPT_STEP = 10

BETA_ONE = 0.9
BETA_TWO = 0.95
RATE = 0.02
DECAY = 0.1
EPSILON = 1e-08

BLOCK = 256
SCORE_SCALE = HD**-0.5 * 1.4426950408889634
MESH = pl.DeviceIdType.MESH


def adamw(master, moment_one, moment_two, grads):
    first_moment = BETA_ONE * moment_one + (1.0 - BETA_ONE) * grads
    second_moment = BETA_TWO * moment_two + (1.0 - BETA_TWO) * grads * grads
    first_hat = first_moment / (1.0 - BETA_ONE**OPT_STEP)
    second_hat = second_moment / (1.0 - BETA_TWO**OPT_STEP)
    updated = master - RATE * (first_hat / (jnp.sqrt(second_hat) + EPSILON) + DECAY * master)
    return (updated, first_moment, second_moment)


def normalize(values, gain, bias):
    values = values.astype(jnp.float32)
    centred = values - jnp.mean(values, axis=-1, keepdims=True)
    spread = jnp.mean(centred * centred, axis=-1, keepdims=True)
    return (centred / jnp.sqrt(spread + 1e-06) * gain + bias).astype(jnp.bfloat16)


def attend(queries, keys, values):
    scores = lax.dot_general(
        queries, keys, (((1,), (1,)), ((), ())), preferred_element_type=jnp.float32
    )
    top = jnp.max(scores, axis=-1, keepdims=True)
    weights = jnp.exp2((scores - top) * SCORE_SCALE)
    total = jnp.sum(weights, axis=-1, keepdims=True)
    probs = (weights * (1.0 / total)).astype(jnp.bfloat16)
    out = jnp.dot(probs, values, preferred_element_type=jnp.float32)
    return out.astype(jnp.bfloat16)


def peer(step, me):
    turn = step // 4
    hops = (12 + (turn + 1) // 2 * (1 - 2 * (turn % 2))) % 8
    half = (me // 16 + 1 - (step // 2) % 2) % 2
    row = (me // 2 % 8 + hops) % 8
    core = (me + 1 - step % 2) % 2
    return half * 16 + row * 2 + core


def kernel(groups, replicas, qkv, layer, out, got, keys, queries, done, gains, in_sem, in_sent, out_sem, out_sent, gain_sem, gain_sent):
    samples, rows = qkv.shape[2], qkv.shape[3]
    patches = rows * groups
    me = lax.axis_index("seq")
    replica = lax.axis_index("dp")
    owner = me * HD // layer.shape[1]

    barrier = pltpu.get_barrier_semaphore()

    def greet_seq(step, carry):
        pl.semaphore_signal(barrier, 1, device_id=(replica, peer(step, me)), device_id_type=MESH)
        return carry

    def greet_dp(step, carry):
        pl.semaphore_signal(
            barrier, 1, device_id=((replica + step) % replicas, me), device_id_type=MESH
        )
        return carry

    lax.fori_loop(0, groups - 1, greet_seq, 0)
    lax.fori_loop(1, replicas, greet_dp, 0)
    pl.semaphore_wait(barrier, groups - 1 + replicas - 1)

    own_layer = layer.at[:, pl.ds(pl.multiple_of(me * HD % layer.shape[1], HD), HD)]

    @pl.when(replica == owner)
    def _():
        def give(step, carry):
            pltpu.make_async_remote_copy(
                own_layer,
                gains,
                gain_sent,
                gain_sem,
                device_id=((replica + step) % replicas, me),
                device_id_type=MESH,
            ).start()
            return carry

        lax.fori_loop(1, replicas, give, 0)
        pltpu.make_async_copy(own_layer, gains, gain_sem).start()

    mine = pl.ds(pl.multiple_of(me * rows, rows), rows)

    def slice_of(first, count, sample, device):
        columns = pl.ds(pl.multiple_of(device * HD, HD), HD)
        return qkv.at[pl.ds(first, count), 0, sample, :, columns]

    for sample in range(samples):
        for part, (first, count) in enumerate(((1, 2), (0, 1))):
            target = got.at[sample, pl.ds(first, count), mine, :]

            def send(step, carry):
                device = peer(step, me)
                pltpu.make_async_remote_copy(
                    slice_of(first, count, sample, device),
                    target,
                    in_sent.at[sample, part],
                    in_sem.at[sample, part],
                    device_id=(replica, device),
                    device_id_type=MESH,
                ).start()
                return carry

            lax.fori_loop(0, groups - 1, send, 0)
            pltpu.make_async_copy(
                slice_of(first, count, sample, me), target, in_sem.at[sample, part]
            ).start()

    pltpu.make_async_copy(gains, gains, gain_sem).wait()
    table = gains[...].astype(jnp.float32)

    out_columns = pl.ds(pl.multiple_of(me * HD, HD), HD)
    sharers = BLOCK // rows
    blocks = patches // BLOCK
    for sample in range(samples):
        for part, (first, count) in enumerate(((1, 2), (0, 1))):
            whole = got.at[sample, pl.ds(first, count)]
            pltpu.make_async_copy(whole, whole, in_sem.at[sample, part]).wait()
            source = got.at[sample, first]
            target = keys if part == 0 else queries
            gain, bias = (table[2:3], table[3:4]) if part == 0 else (table[0:1], table[1:2])

            def norm_rows(step, carry):
                at = pl.ds(pl.multiple_of(step * BLOCK, BLOCK), BLOCK)
                target[at, :] = normalize(source[at, :], gain, bias)
                return carry

            lax.fori_loop(0, blocks, norm_rows, 0)

        def one_block(step, carry):
            block = (me // sharers + step) % blocks
            at = pl.ds(pl.multiple_of(block * BLOCK, BLOCK), BLOCK)
            done[sample, at, :] = attend(queries[at, :], keys[...], got[sample, 2])
            for share in range(sharers):
                device = block * sharers + share
                source = done.at[sample, pl.ds(pl.multiple_of(device * rows, rows), rows), :]
                target = out.at[0, sample, :, out_columns]

                @pl.when(device != me)
                def _():
                    pltpu.make_async_remote_copy(
                        source,
                        target,
                        out_sent,
                        out_sem,
                        device_id=(replica, device),
                        device_id_type=MESH,
                    ).start()

                @pl.when(device == me)
                def _():
                    pltpu.make_async_copy(source, target, out_sem).start()

            return carry

        lax.fori_loop(0, blocks, one_block, 0)

    others = rows * (groups - 1)
    for sample in range(samples):
        for part, (first, count) in enumerate(((1, 2), (0, 1))):
            sent = got.at[sample, pl.ds(first, count), pl.ds(0, others)]
            pltpu.make_async_copy(sent, sent, in_sent.at[sample, part]).wait()
    sent = done.at[:, pl.ds(0, others)]
    pltpu.make_async_copy(sent, sent, out_sent).wait()
    pltpu.make_async_copy(out, out, out_sem).wait()

    @pl.when(replica == owner)
    def _():
        def gave(step, carry):
            pltpu.make_async_copy(gains, gains, gain_sent).wait()
            return carry

        lax.fori_loop(1, replicas, gave, 0)


def shards(qkv, master, moment_one, moment_two, grads):
    updated, first_moment, second_moment = adamw(master, moment_one, moment_two, grads)
    layer = updated.astype(jnp.bfloat16)
    groups = lax.axis_size("seq")
    replicas = lax.axis_size("dp")
    _, _, samples, rows, width = qkv.shape
    patches = rows * groups
    attended = pl.pallas_call(
        functools.partial(kernel, groups, replicas),
        out_shape=jax.ShapeDtypeStruct((1, samples, rows, width), jnp.bfloat16),
        in_specs=[pl.BlockSpec(memory_space=pl.ANY), pl.BlockSpec(memory_space=pltpu.VMEM)],
        out_specs=pl.BlockSpec(memory_space=pl.ANY),
        scratch_shapes=[
            pltpu.VMEM((samples, 3, patches, HD), jnp.bfloat16),
            pltpu.VMEM((patches, HD), jnp.bfloat16),
            pltpu.VMEM((patches, HD), jnp.bfloat16),
            pltpu.VMEM((samples, patches, HD), jnp.bfloat16),
            pltpu.VMEM((4, HD), jnp.bfloat16),
            pltpu.SemaphoreType.DMA((samples, 2)),
            pltpu.SemaphoreType.DMA((samples, 2)),
            pltpu.SemaphoreType.DMA,
            pltpu.SemaphoreType.DMA,
            pltpu.SemaphoreType.DMA,
            pltpu.SemaphoreType.DMA,
        ],
        compiler_params=pltpu.CompilerParams(
            collective_id=0, has_side_effects=True, vmem_limit_bytes=48 * 1024 * 1024
        ),
    )(qkv, layer)
    return (attended, updated, first_moment, second_moment)


def solution(mesh):
    placed = (
        P(None, "dp", None, "seq", None),
        P(None, "dp"),
        P(None, "dp"),
        P(None, "dp"),
        P(None, "dp"),
    )
    return jax.shard_map(
        shards,
        mesh=mesh,
        in_specs=placed,
        out_specs=(P("dp", None, "seq", None), P(None, "dp"), P(None, "dp"), P(None, "dp")),
        check_vma=False,
    )
```

```python
import functools

import jax
import jax.numpy as jnp
from jax import lax
from jax.experimental import pallas as pl
from jax.experimental.pallas import tpu as pltpu
from jax.sharding import PartitionSpec as P

HEADS = 32
HD = 128
OPT_STEP = 10

BETA_ONE = 0.9
BETA_TWO = 0.95
RATE = 0.02
DECAY = 0.1
EPSILON = 1e-08

BLOCK = 256
SCORE_SCALE = HD**-0.5 * 1.4426950408889634
MESH = pl.DeviceIdType.MESH


def adamw(master, moment_one, moment_two, grads):
    first_moment = BETA_ONE * moment_one + (1.0 - BETA_ONE) * grads
    second_moment = BETA_TWO * moment_two + (1.0 - BETA_TWO) * grads * grads
    first_hat = first_moment / (1.0 - BETA_ONE**OPT_STEP)
    second_hat = second_moment / (1.0 - BETA_TWO**OPT_STEP)
    updated = master - RATE * (first_hat / (jnp.sqrt(second_hat) + EPSILON) + DECAY * master)
    return (updated, first_moment, second_moment)


def normalize(values, gain, bias):
    values = values.astype(jnp.float32)
    centred = values - jnp.mean(values, axis=-1, keepdims=True)
    spread = jnp.mean(centred * centred, axis=-1, keepdims=True)
    return (centred / jnp.sqrt(spread + 1e-06) * gain + bias).astype(jnp.bfloat16)


def attend(queries, keys, values):
    scores = lax.dot_general(
        queries, keys, (((1,), (1,)), ((), ())), preferred_element_type=jnp.float32
    )
    top = jnp.max(scores, axis=-1, keepdims=True)
    weights = jnp.exp2((scores - top) * SCORE_SCALE)
    total = jnp.sum(weights, axis=-1, keepdims=True)
    probs = (weights * (1.0 / total)).astype(jnp.bfloat16)
    out = jnp.dot(probs, values, preferred_element_type=jnp.float32)
    return out.astype(jnp.bfloat16)


def loop(count, body):
    def step(index, carry):
        body(index)
        return carry

    lax.fori_loop(0, count, step, 0)


def kernel(groups, replicas, qkv, layer, out, got, by_row, by_half, keys, done, relay, gains,
           got_sem, late_sem, row_sem, half_sem, relay_sem, out_sem, gain_sem,
           near_sent, row_sent, half_sent, out_sent, relay_sent, gain_sent):
    samples, rows = qkv.shape[2], qkv.shape[3]
    half_size = groups // 2
    chips = half_size // 2
    half_rows = rows * half_size
    me = lax.axis_index("seq")
    replica = lax.axis_index("dp")
    half, place = me // half_size, me % half_size
    chip, core = place // 2, place % 2
    opposite = (me + half_size) % groups
    owner = me * HD // layer.shape[1]

    def hops(turn):
        return (chips + chips // 2 + (turn + 1) // 2 * (1 - 2 * (turn % 2))) % chips

    def peer(step):
        return (chip + hops(step // 2)) % chips * 2 + (core + 1 - step % 2) % 2

    def at_rows(device):
        return pl.ds(pl.multiple_of(device * rows, rows), rows)

    def columns(device, count=1):
        return pl.ds(pl.multiple_of(device * HD, HD), count * HD)

    def push(source, target, sent, arrived, device):
        pltpu.make_async_remote_copy(
            source, target, sent, arrived, device_id=(replica, device), device_id_type=MESH
        ).start()

    def keep(source, target, arrived):
        pltpu.make_async_copy(source, target, arrived).start()

    def wait(ref, semaphore):
        pltpu.make_async_copy(ref, ref, semaphore).wait()

    Q, K, V = 0, 1, 2
    pair = 2 * rows
    turns = chips // 2

    def spots(turn):
        distance = turns - turn
        return (chip + distance) % chips, (chip + chips - distance % turns) % chips

    def chip_rows(which, seat):
        return pl.ds(pl.multiple_of(which * half_rows + seat * pair, pair), pair)

    barrier = pltpu.get_barrier_semaphore()

    def greet_row(step, carry):
        device = half * half_size + peer(step)
        pl.semaphore_signal(barrier, 1, device_id=(replica, device), device_id_type=MESH)
        return carry

    def greet_dp(step, carry):
        other = (replica + step) % replicas
        pl.semaphore_signal(barrier, 1, device_id=(other, me), device_id_type=MESH)
        return carry

    lax.fori_loop(0, half_size - 1, greet_row, 0)
    pl.semaphore_signal(barrier, 1, device_id=(replica, opposite), device_id_type=MESH)
    lax.fori_loop(1, replicas, greet_dp, 0)
    pl.semaphore_wait(barrier, half_size - 1 + 1 + replicas - 1)

    own_layer = layer.at[:, pl.ds(pl.multiple_of(me * HD % layer.shape[1], HD), HD)]

    @pl.when(replica == owner)
    def _():
        def give(step, carry):
            pltpu.make_async_remote_copy(
                own_layer,
                gains,
                gain_sent,
                gain_sem,
                device_id=((replica + step) % replicas, me),
                device_id_type=MESH,
            ).start()
            return carry

        lax.fori_loop(1, replicas, give, 0)
        keep(own_layer, gains, gain_sem)

    def near(sample, part):
        target = got.at[sample, part, at_rows(me), :]
        arrived = got_sem.at[sample, part]

        def send(step, carry):
            device = half * half_size + peer(step)
            source = qkv.at[part, 0, sample, :, columns(device)]
            push(source, target, near_sent.at[sample, part], arrived, device)
            return carry

        lax.fori_loop(0, half_size - 1, send, 0)
        keep(qkv.at[part, 0, sample, :, columns(me)], target, arrived)

    def row_first(sample, part, slot):
        target = by_row.at[slot, at_rows(place), :]

        def send(step, carry):
            seat = peer(step)
            source = qkv.at[part, 0, sample, :, columns((1 - half) * half_size + seat)]
            push(source, target, row_sent.at[slot], row_sem.at[slot], half * half_size + seat)
            return carry

        lax.fori_loop(0, half_size - 1, send, 0)
        source = qkv.at[part, 0, sample, :, columns(opposite)]
        keep(source, target, row_sem.at[slot])

    def row_then_half(sample, part, slot):
        wait(by_row.at[slot], row_sem.at[slot])
        at = pl.ds(pl.multiple_of(half * half_rows, half_rows), half_rows)
        push(
            by_row.at[slot], got.at[sample, part, at, :], half_sent.at[slot],
            got_sem.at[sample, part], opposite,
        )

    def row_then_half_by_turn(sample, part, slot):
        wait(by_row.at[slot], row_sem.at[slot])

        def send(turn):
            for seat in spots(turn):
                source = by_row.at[slot, pl.ds(pl.multiple_of(seat * pair, pair), pair), :]
                target = got.at[sample, part, chip_rows(half, seat), :]
                push(source, target, half_sent.at[slot], late_sem.at[turn], opposite)

        loop(turns, send)

    def half_first(sample, part, slot):
        source = qkv.at[part, 0, sample, :, columns((1 - half) * half_size, half_size)]
        push(source, by_half.at[slot], half_sent.at[3 + slot], half_sem.at[slot], opposite)

    def half_then_row(sample, part, slot):
        wait(by_half.at[slot], half_sem.at[slot])
        target = got.at[sample, part, at_rows(opposite), :]
        arrived = got_sem.at[sample, part]

        def send(step, carry):
            seat = peer(step)
            source = by_half.at[slot, :, columns(seat)]
            push(source, target, row_sent.at[3 + slot], arrived, half * half_size + seat)
            return carry

        lax.fori_loop(0, half_size - 1, send, 0)
        keep(by_half.at[slot, :, columns(place)], target, arrived)

    def norm_keys(sample):
        wait(got.at[sample, K], got_sem.at[sample, K])

        def norm_rows(step):
            at = pl.ds(pl.multiple_of(step * BLOCK, BLOCK), BLOCK)
            keys[sample, at, :] = normalize(got[sample, K, at, :], table[2:3], table[3:4])

        loop(keys.shape[1] // BLOCK, norm_rows)

    def attend_turn(sample, turn, which):
        ats = [chip_rows(which, seat) for seat in spots(turn)]
        block = jnp.concatenate([got[sample, Q, at, :] for at in ats], axis=0)
        queries = normalize(block, table[0:1], table[1:2])
        return attend(queries, keys[sample], got[sample, V])

    def far_turn(sample, turn):
        done[sample, 0, turn] = attend_turn(sample, turn, 1 - half)

    def send_far(sample, turn):
        push(
            done.at[sample, 0, turn], relay.at[sample, turn], out_sent.at[0],
            relay_sem.at[sample, turn], opposite,
        )

    def hand_out(source, head, sample, turn, sent):
        target = out.at[0, sample, :, columns(head)]
        for side, seat in enumerate(spots(turn)):
            for unit in range(2):
                piece = source.at[pl.ds(side * pair + unit * rows, rows), :]
                device = half * half_size + seat * 2 + unit

                @pl.when(device != me)
                def _():
                    push(piece, target, sent, out_sem, device)

                @pl.when(device == me)
                def _():
                    keep(piece, target, out_sem)

    def near_turn(sample, turn):
        done[sample, 1, turn] = attend_turn(sample, turn, half)
        hand_out(done.at[sample, 1, turn], me, sample, turn, out_sent.at[1])

    def relay_turn(sample, turn):
        wait(relay.at[sample, turn], relay_sem.at[sample, turn])
        hand_out(relay.at[sample, turn], opposite, sample, turn, relay_sent)

    half_first(0, K, 0)
    row_first(1, K, 0)
    near(0, K)
    half_first(0, V, 1)
    near(0, V)
    near(0, Q)
    half_then_row(0, K, 0)
    half_first(0, Q, 2)
    half_then_row(0, V, 1)
    row_then_half(1, K, 0)
    row_first(1, V, 1)
    half_then_row(0, Q, 2)
    row_first(1, Q, 2)
    row_then_half(1, V, 1)

    wait(gains, gain_sem)
    table = gains[...].astype(jnp.float32)
    norm_keys(0)
    wait(got.at[0, V], got_sem.at[0, V])
    row_then_half_by_turn(1, Q, 2)
    near(1, K)
    wait(got.at[0, Q], got_sem.at[0, Q])
    near(1, V)
    near(1, Q)
    loop(turns, lambda turn: far_turn(0, turn))
    loop(turns, lambda turn: near_turn(0, turn))
    norm_keys(1)
    wait(got.at[1, V], got_sem.at[1, V])
    loop(turns, lambda turn: send_far(0, turn))
    wait(got.at[1, Q, pl.ds(0, half_rows)], got_sem.at[1, Q])
    loop(turns, lambda turn: near_turn(1, turn))

    def late_turn(turn):
        wait(got.at[1, Q, pl.ds(0, 2 * pair)], late_sem.at[turn])
        far_turn(1, turn)
        send_far(1, turn)

    loop(turns, late_turn)
    loop(turns, lambda turn: relay_turn(0, turn))
    loop(turns, lambda turn: relay_turn(1, turn))

    others = rows * (half_size - 1)
    for sample in range(samples):
        for part in range(3):
            wait(got.at[sample, part, pl.ds(0, others)], near_sent.at[sample, part])
    for slot in range(6):
        wait(by_row.at[0, pl.ds(0, others)], row_sent.at[slot])
        wait(by_row.at[0], half_sent.at[slot])
    wait(done.at[:, 0], out_sent.at[0])
    wait(got.at[0, pl.ds(0, 2), pl.ds(0, others)], out_sent.at[1])
    wait(got.at[0, pl.ds(0, 2), pl.ds(0, others)], relay_sent)
    wait(out, out_sem)

    @pl.when(replica == owner)
    def _():
        loop(replicas - 1, lambda step: wait(gains, gain_sent))


def shards(qkv, master, moment_one, moment_two, grads):
    updated, first_moment, second_moment = adamw(master, moment_one, moment_two, grads)
    layer = updated.astype(jnp.bfloat16)
    groups = lax.axis_size("seq")
    replicas = lax.axis_size("dp")
    _, _, samples, rows, width = qkv.shape
    patches = rows * groups
    attended = pl.pallas_call(
        functools.partial(kernel, groups, replicas),
        out_shape=jax.ShapeDtypeStruct((1, samples, rows, width), jnp.bfloat16),
        in_specs=[pl.BlockSpec(memory_space=pl.ANY), pl.BlockSpec(memory_space=pltpu.VMEM)],
        out_specs=pl.BlockSpec(memory_space=pl.ANY),
        scratch_shapes=[
            pltpu.VMEM((samples, 3, patches, HD), jnp.bfloat16),
            pltpu.VMEM((3, patches // 2, HD), jnp.bfloat16),
            pltpu.VMEM((3, rows, groups // 2 * HD), jnp.bfloat16),
            pltpu.VMEM((samples, patches, HD), jnp.bfloat16),
            pltpu.VMEM((samples, 2, groups // 8, 4 * rows, HD), jnp.bfloat16),
            pltpu.VMEM((samples, groups // 8, 4 * rows, HD), jnp.bfloat16),
            pltpu.VMEM((4, HD), jnp.bfloat16),
            pltpu.SemaphoreType.DMA((samples, 3)),
            pltpu.SemaphoreType.DMA((groups // 8,)),
            pltpu.SemaphoreType.DMA((3,)),
            pltpu.SemaphoreType.DMA((3,)),
            pltpu.SemaphoreType.DMA((samples, groups // 8)),
            pltpu.SemaphoreType.DMA,
            pltpu.SemaphoreType.DMA,
            pltpu.SemaphoreType.DMA((samples, 3)),
            pltpu.SemaphoreType.DMA((6,)),
            pltpu.SemaphoreType.DMA((6,)),
            pltpu.SemaphoreType.DMA((2,)),
            pltpu.SemaphoreType.DMA,
            pltpu.SemaphoreType.DMA,
        ],
        compiler_params=pltpu.CompilerParams(
            collective_id=0, has_side_effects=True, vmem_limit_bytes=48 * 1024 * 1024
        ),
    )(qkv, layer)
    return (attended, updated, first_moment, second_moment)


def solution(mesh):
    placed = (
        P(None, "dp", None, "seq", None),
        P(None, "dp"),
        P(None, "dp"),
        P(None, "dp"),
        P(None, "dp"),
    )
    return jax.shard_map(
        shards,
        mesh=mesh,
        in_specs=placed,
        out_specs=(P("dp", None, "seq", None), P(None, "dp"), P(None, "dp"), P(None, "dp")),
        check_vma=False,
    )
```

```python
import functools

import jax
import jax.numpy as jnp
from jax import lax
from jax.experimental import pallas as pl
from jax.experimental.pallas import tpu as pltpu
from jax.sharding import PartitionSpec as P

HEADS = 32
HD = 128
OPT_STEP = 10

BETA_ONE = 0.9
BETA_TWO = 0.95
RATE = 0.02
DECAY = 0.1
EPSILON = 1e-08

BLOCK = 256
SCORE_SCALE = HD**-0.5 * 1.4426950408889634
MESH = pl.DeviceIdType.MESH


def adamw(master, moment_one, moment_two, grads):
    first_moment = BETA_ONE * moment_one + (1.0 - BETA_ONE) * grads
    second_moment = BETA_TWO * moment_two + (1.0 - BETA_TWO) * grads * grads
    first_hat = first_moment / (1.0 - BETA_ONE**OPT_STEP)
    second_hat = second_moment / (1.0 - BETA_TWO**OPT_STEP)
    updated = master - RATE * (first_hat / (jnp.sqrt(second_hat) + EPSILON) + DECAY * master)
    return (updated, first_moment, second_moment)


def normalize(values, gain, bias):
    values = values.astype(jnp.float32)
    centred = values - jnp.mean(values, axis=-1, keepdims=True)
    spread = jnp.mean(centred * centred, axis=-1, keepdims=True)
    return (centred / jnp.sqrt(spread + 1e-06) * gain + bias).astype(jnp.bfloat16)


def attend(queries, keys, values):
    scores = lax.dot_general(
        queries, keys, (((1,), (1,)), ((), ())), preferred_element_type=jnp.float32
    )
    top = jnp.max(scores, axis=-1, keepdims=True)
    weights = jnp.exp2((scores - top) * SCORE_SCALE)
    total = jnp.sum(weights, axis=-1, keepdims=True)
    probs = (weights * (1.0 / total)).astype(jnp.bfloat16)
    out = jnp.dot(probs, values, preferred_element_type=jnp.float32)
    return out.astype(jnp.bfloat16)


def loop(count, body):
    def step(index, carry):
        body(index)
        return carry

    lax.fori_loop(0, count, step, 0)


def kernel(groups, replicas, stored, layer, out, qkv, got, by_row, by_half, keys, done, relay, gains,
           load_sem, got_sem, late_sem, row_sem, half_sem, relay_sem, out_sem, gain_sem,
           near_sent, row_sent, half_sent, out_sent, relay_sent, gain_sent):
    samples, rows = stored.shape[2], stored.shape[3]
    half_size = groups // 2
    chips = half_size // 2
    half_rows = rows * half_size
    me = lax.axis_index("seq")
    replica = lax.axis_index("dp")
    half, place = me // half_size, me % half_size
    chip, core = place // 2, place % 2
    opposite = (me + half_size) % groups
    owner = me * HD // layer.shape[1]

    def hops(turn):
        return (chips + chips // 2 + (turn + 1) // 2 * (1 - 2 * (turn % 2))) % chips

    def peer(step):
        return (chip + hops(step // 2)) % chips * 2 + (core + 1 - step % 2) % 2

    def at_rows(device):
        return pl.ds(pl.multiple_of(device * rows, rows), rows)

    def columns(device, count=1):
        return pl.ds(pl.multiple_of(device * HD, HD), count * HD)

    def push(source, target, sent, arrived, device):
        pltpu.make_async_remote_copy(
            source, target, sent, arrived, device_id=(replica, device), device_id_type=MESH
        ).start()

    def keep(source, target, arrived):
        pltpu.make_async_copy(source, target, arrived).start()

    def wait(ref, semaphore):
        pltpu.make_async_copy(ref, ref, semaphore).wait()

    Q, K, V = 0, 1, 2
    pair = 2 * rows
    turns = chips // 2

    def spots(turn):
        distance = turns - turn
        return (chip + distance) % chips, (chip + chips - distance % turns) % chips

    def chip_rows(which, seat):
        return pl.ds(pl.multiple_of(which * half_rows + seat * pair, pair), pair)

    for sample, part in ((0, K), (1, K), (0, V), (0, Q), (1, V), (1, Q)):
        keep(stored.at[part, 0, sample], qkv.at[part, 0, sample], load_sem.at[sample, part])

    def loaded(sample, part):
        wait(qkv.at[part, 0, sample], load_sem.at[sample, part])

    barrier = pltpu.get_barrier_semaphore()

    def greet_row(step, carry):
        device = half * half_size + peer(step)
        pl.semaphore_signal(barrier, 1, device_id=(replica, device), device_id_type=MESH)
        return carry

    def greet_dp(step, carry):
        other = (replica + step) % replicas
        pl.semaphore_signal(barrier, 1, device_id=(other, me), device_id_type=MESH)
        return carry

    pl.semaphore_signal(barrier, 1, device_id=(replica, opposite), device_id_type=MESH)
    lax.fori_loop(0, half_size - 1, greet_row, 0)
    lax.fori_loop(1, replicas, greet_dp, 0)
    pl.semaphore_wait(barrier, half_size - 1 + 1 + replicas - 1)

    own_layer = layer.at[:, pl.ds(pl.multiple_of(me * HD % layer.shape[1], HD), HD)]

    def near(sample, part):
        target = got.at[sample, part, at_rows(me), :]
        arrived = got_sem.at[sample, part]

        def send(step, carry):
            device = half * half_size + peer(step)
            source = qkv.at[part, 0, sample, :, columns(device)]
            push(source, target, near_sent.at[sample, part], arrived, device)
            return carry

        lax.fori_loop(0, half_size - 1, send, 0)
        keep(qkv.at[part, 0, sample, :, columns(me)], target, arrived)

    def row_first(sample, part, slot):
        target = by_row.at[slot, at_rows(place), :]

        def send(step, carry):
            seat = peer(step)
            source = qkv.at[part, 0, sample, :, columns((1 - half) * half_size + seat)]
            push(source, target, row_sent.at[slot], row_sem.at[slot], half * half_size + seat)
            return carry

        lax.fori_loop(0, half_size - 1, send, 0)
        source = qkv.at[part, 0, sample, :, columns(opposite)]
        keep(source, target, row_sem.at[slot])

    def row_then_half(sample, part, slot):
        wait(by_row.at[slot], row_sem.at[slot])
        at = pl.ds(pl.multiple_of(half * half_rows, half_rows), half_rows)
        push(
            by_row.at[slot], got.at[sample, part, at, :], half_sent.at[slot],
            got_sem.at[sample, part], opposite,
        )

    def row_then_half_by_turn(sample, part, slot):
        wait(by_row.at[slot], row_sem.at[slot])

        def send(turn):
            for seat in spots(turn):
                source = by_row.at[slot, pl.ds(pl.multiple_of(seat * pair, pair), pair), :]
                target = got.at[sample, part, chip_rows(half, seat), :]
                push(source, target, half_sent.at[slot], late_sem.at[turn], opposite)

        loop(turns, send)

    def half_first(sample, part, slot):
        source = qkv.at[part, 0, sample, :, columns((1 - half) * half_size, half_size)]
        push(source, by_half.at[slot], half_sent.at[3 + slot], half_sem.at[slot], opposite)

    def half_then_row(sample, part, slot):
        target = got.at[sample, part, at_rows(opposite), :]
        arrived = got_sem.at[sample, part]

        def send(step, carry):
            seat = peer(step)
            source = by_half.at[slot, :, columns(seat)]
            push(source, target, row_sent.at[3 + slot], arrived, half * half_size + seat)
            return carry

        lax.fori_loop(0, half_size - 1, send, 0)
        keep(by_half.at[slot, :, columns(place)], target, arrived)

    def norm_keys(sample):
        wait(got.at[sample, K], got_sem.at[sample, K])

        def norm_rows(step):
            at = pl.ds(pl.multiple_of(step * BLOCK, BLOCK), BLOCK)
            keys[sample, at, :] = normalize(got[sample, K, at, :], table[2:3], table[3:4])

        loop(keys.shape[1] // BLOCK, norm_rows)

    def attend_turn(sample, turn, which):
        ats = [chip_rows(which, seat) for seat in spots(turn)]
        block = jnp.concatenate([got[sample, Q, at, :] for at in ats], axis=0)
        queries = normalize(block, table[0:1], table[1:2])
        return attend(queries, keys[sample], got[sample, V])

    def far_turn(sample, turn):
        done[sample, 0, turn] = attend_turn(sample, turn, 1 - half)

    def send_far(sample, turn):
        push(
            done.at[sample, 0, turn], relay.at[sample, turn], out_sent.at[0],
            relay_sem.at[sample, turn], opposite,
        )

    def hand_out(source, head, sample, turn, sent):
        target = out.at[0, sample, :, columns(head)]
        for side, seat in enumerate(spots(turn)):
            for unit in range(2):
                piece = source.at[pl.ds(side * pair + unit * rows, rows), :]
                device = half * half_size + seat * 2 + unit

                @pl.when(device != me)
                def _():
                    push(piece, target, sent, out_sem, device)

                @pl.when(device == me)
                def _():
                    keep(piece, target, out_sem)

    def near_turn(sample, turn):
        done[sample, 1, turn] = attend_turn(sample, turn, half)
        hand_out(done.at[sample, 1, turn], me, sample, turn, out_sent.at[1])

    def relay_turn(sample, turn):
        wait(relay.at[sample, turn], relay_sem.at[sample, turn])
        hand_out(relay.at[sample, turn], opposite, sample, turn, relay_sent)

    loaded(0, K)
    half_first(0, K, 0)
    loaded(1, K)
    row_first(1, K, 0)
    loaded(0, V)
    half_first(0, V, 1)
    near(0, K)
    near(0, V)
    loaded(0, Q)
    near(0, Q)

    @pl.when(replica == owner)
    def _():
        def give(step, carry):
            pltpu.make_async_remote_copy(
                own_layer,
                gains,
                gain_sent,
                gain_sem,
                device_id=((replica + step) % replicas, me),
                device_id_type=MESH,
            ).start()
            return carry

        lax.fori_loop(1, replicas, give, 0)
        keep(own_layer, gains, gain_sem)

    wait(by_half.at[0], half_sem.at[0])
    half_first(0, Q, 2)
    half_then_row(0, K, 0)
    wait(by_half.at[1], half_sem.at[1])
    row_then_half(1, K, 0)
    half_then_row(0, V, 1)
    loaded(1, V)
    row_first(1, V, 1)
    wait(by_half.at[2], half_sem.at[2])
    row_then_half(1, V, 1)
    half_then_row(0, Q, 2)
    loaded(1, Q)
    row_first(1, Q, 2)

    wait(gains, gain_sem)
    table = gains[...].astype(jnp.float32)
    norm_keys(0)
    wait(got.at[0, V], got_sem.at[0, V])
    row_then_half_by_turn(1, Q, 2)
    near(1, K)
    wait(got.at[0, Q], got_sem.at[0, Q])
    near(1, V)
    near(1, Q)
    loop(turns, lambda turn: far_turn(0, turn))
    loop(turns, lambda turn: near_turn(0, turn))
    norm_keys(1)
    wait(got.at[1, V], got_sem.at[1, V])
    loop(turns, lambda turn: send_far(0, turn))
    wait(got.at[1, Q, pl.ds(0, half_rows)], got_sem.at[1, Q])
    loop(turns, lambda turn: near_turn(1, turn))

    def late_turn(turn):
        wait(got.at[1, Q, pl.ds(0, 2 * pair)], late_sem.at[turn])
        far_turn(1, turn)
        send_far(1, turn)

    loop(turns, late_turn)
    loop(turns, lambda turn: relay_turn(0, turn))
    loop(turns, lambda turn: relay_turn(1, turn))

    others = rows * (half_size - 1)
    for sample in range(samples):
        for part in range(3):
            wait(got.at[sample, part, pl.ds(0, others)], near_sent.at[sample, part])
    for slot in range(6):
        wait(by_row.at[0, pl.ds(0, others)], row_sent.at[slot])
        wait(by_row.at[0], half_sent.at[slot])
    wait(done.at[:, 0], out_sent.at[0])
    wait(got.at[0, pl.ds(0, 2), pl.ds(0, others)], out_sent.at[1])
    wait(got.at[0, pl.ds(0, 2), pl.ds(0, others)], relay_sent)
    wait(out, out_sem)

    @pl.when(replica == owner)
    def _():
        loop(replicas - 1, lambda step: wait(gains, gain_sent))


def shards(qkv, master, moment_one, moment_two, grads):
    updated, first_moment, second_moment = adamw(master, moment_one, moment_two, grads)
    layer = updated.astype(jnp.bfloat16)
    groups = lax.axis_size("seq")
    replicas = lax.axis_size("dp")
    _, _, samples, rows, width = qkv.shape
    patches = rows * groups
    attended = pl.pallas_call(
        functools.partial(kernel, groups, replicas),
        out_shape=jax.ShapeDtypeStruct((1, samples, rows, width), jnp.bfloat16),
        in_specs=[pl.BlockSpec(memory_space=pltpu.HBM), pl.BlockSpec(memory_space=pltpu.VMEM)],
        out_specs=pl.BlockSpec(memory_space=pl.ANY),
        scratch_shapes=[
            pltpu.VMEM(qkv.shape, jnp.bfloat16),
            pltpu.VMEM((samples, 3, patches, HD), jnp.bfloat16),
            pltpu.VMEM((3, patches // 2, HD), jnp.bfloat16),
            pltpu.VMEM((3, rows, groups // 2 * HD), jnp.bfloat16),
            pltpu.VMEM((samples, patches, HD), jnp.bfloat16),
            pltpu.VMEM((samples, 2, groups // 8, 4 * rows, HD), jnp.bfloat16),
            pltpu.VMEM((samples, groups // 8, 4 * rows, HD), jnp.bfloat16),
            pltpu.VMEM((4, HD), jnp.bfloat16),
            pltpu.SemaphoreType.DMA((samples, 3)),
            pltpu.SemaphoreType.DMA((samples, 3)),
            pltpu.SemaphoreType.DMA((groups // 8,)),
            pltpu.SemaphoreType.DMA((3,)),
            pltpu.SemaphoreType.DMA((3,)),
            pltpu.SemaphoreType.DMA((samples, groups // 8)),
            pltpu.SemaphoreType.DMA,
            pltpu.SemaphoreType.DMA,
            pltpu.SemaphoreType.DMA((samples, 3)),
            pltpu.SemaphoreType.DMA((6,)),
            pltpu.SemaphoreType.DMA((6,)),
            pltpu.SemaphoreType.DMA((2,)),
            pltpu.SemaphoreType.DMA,
            pltpu.SemaphoreType.DMA,
        ],
        compiler_params=pltpu.CompilerParams(
            collective_id=0, has_side_effects=True, vmem_limit_bytes=60 * 1024 * 1024
        ),
    )(qkv, layer)
    return (attended, updated, first_moment, second_moment)


def solution(mesh):
    placed = (
        P(None, "dp", None, "seq", None),
        P(None, "dp"),
        P(None, "dp"),
        P(None, "dp"),
        P(None, "dp"),
    )
    return jax.shard_map(
        shards,
        mesh=mesh,
        in_specs=placed,
        out_specs=(P("dp", None, "seq", None), P(None, "dp"), P(None, "dp"), P(None, "dp")),
        check_vma=False,
    )
```

```python
import functools

import jax
import jax.numpy as jnp
from jax import lax
from jax.experimental import pallas as pl
from jax.experimental.pallas import tpu as pltpu
from jax.sharding import PartitionSpec as P

HEADS = 32
HD = 128
OPT_STEP = 10

BETA_ONE = 0.9
BETA_TWO = 0.95
RATE = 0.02
DECAY = 0.1
EPSILON = 1e-08

BLOCK = 256
SCORE_SCALE = HD**-0.5 * 1.4426950408889634
MESH = pl.DeviceIdType.MESH


def adamw(master, moment_one, moment_two, grads):
    first_moment = BETA_ONE * moment_one + (1.0 - BETA_ONE) * grads
    second_moment = BETA_TWO * moment_two + (1.0 - BETA_TWO) * grads * grads
    first_hat = first_moment / (1.0 - BETA_ONE**OPT_STEP)
    second_hat = second_moment / (1.0 - BETA_TWO**OPT_STEP)
    updated = master - RATE * (first_hat / (jnp.sqrt(second_hat) + EPSILON) + DECAY * master)
    return (updated, first_moment, second_moment)


def normalize(values, gain, bias):
    values = values.astype(jnp.float32)
    centred = values - jnp.mean(values, axis=-1, keepdims=True)
    spread = jnp.mean(centred * centred, axis=-1, keepdims=True)
    return (centred / jnp.sqrt(spread + 1e-06) * gain + bias).astype(jnp.bfloat16)


def attend(queries, keys, values):
    scores = lax.dot_general(
        queries, keys, (((1,), (1,)), ((), ())), preferred_element_type=jnp.float32
    )
    top = jnp.max(scores, axis=-1, keepdims=True)
    weights = jnp.exp2((scores - top) * SCORE_SCALE)
    total = jnp.sum(weights, axis=-1, keepdims=True)
    probs = (weights * (1.0 / total)).astype(jnp.bfloat16)
    out = jnp.dot(probs, values, preferred_element_type=jnp.float32)
    return out.astype(jnp.bfloat16)


def loop(count, body):
    def step(index, carry):
        body(index)
        return carry

    lax.fori_loop(0, count, step, 0)


def kernel(groups, replicas, stored, layer, out, qkv, got, by_row, by_half, keys, done, relay, gains,
           load_sem, got_sem, late_sem, row_sem, half_sem, relay_sem, out_sem, gain_sem,
           near_sent, row_sent, half_sent, out_sent, relay_sent, gain_sent):
    samples, rows = stored.shape[2], stored.shape[3]
    half_size = groups // 2
    chips = half_size // 2
    half_rows = rows * half_size
    me = lax.axis_index("seq")
    replica = lax.axis_index("dp")
    half, place = me // half_size, me % half_size
    chip, core = place // 2, place % 2
    opposite = (me + half_size) % groups
    owner = me * HD // layer.shape[1]

    def hops(turn):
        return (chips + chips // 2 + (turn + 1) // 2 * (1 - 2 * (turn % 2))) % chips

    def peer(step):
        return (chip + hops(step // 2)) % chips * 2 + (core + 1 - step % 2) % 2

    def at_rows(device):
        return pl.ds(pl.multiple_of(device * rows, rows), rows)

    def columns(device, count=1):
        return pl.ds(pl.multiple_of(device * HD, HD), count * HD)

    def push(source, target, sent, arrived, device):
        pltpu.make_async_remote_copy(
            source, target, sent, arrived, device_id=(replica, device), device_id_type=MESH
        ).start()

    def keep(source, target, arrived):
        pltpu.make_async_copy(source, target, arrived).start()

    def wait(ref, semaphore):
        pltpu.make_async_copy(ref, ref, semaphore).wait()

    Q, K, V = 0, 1, 2
    pair = 2 * rows
    turns = chips // 2

    def spots(turn):
        distance = turns - turn
        return (chip + distance) % chips, (chip + chips - distance % turns) % chips

    def chip_rows(which, seat):
        return pl.ds(pl.multiple_of(which * half_rows + seat * pair, pair), pair)

    for sample, part in ((0, K), (1, K), (0, V), (0, Q), (1, V), (1, Q)):
        keep(stored.at[part, 0, sample], qkv.at[part, 0, sample], load_sem.at[sample, part])

    def loaded(sample, part):
        wait(qkv.at[part, 0, sample], load_sem.at[sample, part])

    barrier = pltpu.get_barrier_semaphore()

    def greet_row(step, carry):
        device = half * half_size + peer(step)
        pl.semaphore_signal(barrier, 1, device_id=(replica, device), device_id_type=MESH)
        return carry

    def greet_dp(step, carry):
        other = (replica + step) % replicas
        pl.semaphore_signal(barrier, 1, device_id=(other, me), device_id_type=MESH)
        return carry

    pl.semaphore_signal(barrier, 1, device_id=(replica, opposite), device_id_type=MESH)
    lax.fori_loop(0, half_size - 1, greet_row, 0)
    lax.fori_loop(1, replicas, greet_dp, 0)
    pl.semaphore_wait(barrier, half_size - 1 + 1 + replicas - 1)

    own_layer = layer.at[:, pl.ds(pl.multiple_of(me * HD % layer.shape[1], HD), HD)]

    def near(sample, part):
        target = got.at[sample, part, at_rows(me), :]
        arrived = got_sem.at[sample, part]

        def send(step, carry):
            device = half * half_size + peer(step)
            source = qkv.at[part, 0, sample, :, columns(device)]
            push(source, target, near_sent.at[sample, part], arrived, device)
            return carry

        lax.fori_loop(0, half_size - 1, send, 0)
        keep(qkv.at[part, 0, sample, :, columns(me)], target, arrived)

    def row_first(sample, part, slot):
        target = by_row.at[slot, at_rows(place), :]

        def send(step, carry):
            seat = peer(step)
            source = qkv.at[part, 0, sample, :, columns((1 - half) * half_size + seat)]
            push(source, target, row_sent.at[slot], row_sem.at[slot], half * half_size + seat)
            return carry

        lax.fori_loop(0, half_size - 1, send, 0)
        source = qkv.at[part, 0, sample, :, columns(opposite)]
        keep(source, target, row_sem.at[slot])

    def row_then_half(sample, part, slot):
        wait(by_row.at[slot], row_sem.at[slot])
        at = pl.ds(pl.multiple_of(half * half_rows, half_rows), half_rows)
        push(
            by_row.at[slot], got.at[sample, part, at, :], half_sent.at[slot],
            got_sem.at[sample, part], opposite,
        )

    def row_then_half_by_turn(sample, part, slot):
        wait(by_row.at[slot], row_sem.at[slot])

        def send(turn):
            for seat in spots(turn):
                source = by_row.at[slot, pl.ds(pl.multiple_of(seat * pair, pair), pair), :]
                target = got.at[sample, part, chip_rows(half, seat), :]
                push(source, target, half_sent.at[slot], late_sem.at[turn], opposite)

        loop(turns, send)

    def half_first(sample, part, slot):
        source = qkv.at[part, 0, sample, :, columns((1 - half) * half_size, half_size)]
        push(source, by_half.at[slot], half_sent.at[3 + slot], half_sem.at[slot], opposite)

    def half_then_row(sample, part, slot):
        target = got.at[sample, part, at_rows(opposite), :]
        arrived = got_sem.at[sample, part]

        def send(step, carry):
            seat = peer(step)
            source = by_half.at[slot, :, columns(seat)]
            push(source, target, row_sent.at[3 + slot], arrived, half * half_size + seat)
            return carry

        lax.fori_loop(0, half_size - 1, send, 0)
        keep(by_half.at[slot, :, columns(place)], target, arrived)

    def norm_keys(sample):
        wait(got.at[sample, K], got_sem.at[sample, K])

        def norm_rows(step):
            at = pl.ds(pl.multiple_of(step * BLOCK, BLOCK), BLOCK)
            keys[sample, at, :] = normalize(got[sample, K, at, :], table[2:3], table[3:4])

        loop(keys.shape[1] // BLOCK, norm_rows)

    def attend_turn(sample, turn, which):
        ats = [chip_rows(which, seat) for seat in spots(turn)]
        block = jnp.concatenate([got[sample, Q, at, :] for at in ats], axis=0)
        queries = normalize(block, table[0:1], table[1:2])
        return attend(queries, keys[sample], got[sample, V])

    def far_turn(sample, turn):
        done[sample, 0, turn] = attend_turn(sample, turn, 1 - half)

    def send_far(sample, turn):
        push(
            done.at[sample, 0, turn], relay.at[sample, turn], out_sent.at[0],
            relay_sem.at[sample, turn], opposite,
        )

    def hand_out(source, head, sample, turn, sent):
        target = out.at[0, sample, :, columns(head)]
        for side, seat in enumerate(spots(turn)):
            for unit in range(2):
                piece = source.at[pl.ds(side * pair + unit * rows, rows), :]
                device = half * half_size + seat * 2 + unit

                @pl.when(device != me)
                def _():
                    push(piece, target, sent, out_sem, device)

                @pl.when(device == me)
                def _():
                    keep(piece, target, out_sem)

    def near_turn(sample, turn):
        done[sample, 1, turn] = attend_turn(sample, turn, half)
        hand_out(done.at[sample, 1, turn], me, sample, turn, out_sent.at[1])

    def relay_turn(sample, turn):
        wait(relay.at[sample, turn], relay_sem.at[sample, turn])
        hand_out(relay.at[sample, turn], opposite, sample, turn, relay_sent)

    loaded(0, K)
    half_first(0, K, 0)
    loaded(1, K)
    row_first(1, K, 0)
    loaded(0, V)
    half_first(0, V, 1)
    near(0, K)
    near(0, V)
    loaded(0, Q)
    near(0, Q)

    @pl.when(replica == owner)
    def _():
        def give(step, carry):
            pltpu.make_async_remote_copy(
                own_layer,
                gains,
                gain_sent,
                gain_sem,
                device_id=((replica + step) % replicas, me),
                device_id_type=MESH,
            ).start()
            return carry

        lax.fori_loop(1, replicas, give, 0)
        keep(own_layer, gains, gain_sem)

    wait(by_half.at[0], half_sem.at[0])
    half_first(0, Q, 2)
    half_then_row(0, K, 0)
    wait(by_half.at[1], half_sem.at[1])
    row_then_half(1, K, 0)
    half_then_row(0, V, 1)
    loaded(1, V)
    row_first(1, V, 1)
    wait(by_half.at[2], half_sem.at[2])
    row_then_half(1, V, 1)
    half_then_row(0, Q, 2)
    loaded(1, Q)
    row_first(1, Q, 2)

    wait(gains, gain_sem)
    table = gains[...].astype(jnp.float32)
    norm_keys(0)
    wait(got.at[0, V], got_sem.at[0, V])
    row_then_half_by_turn(1, Q, 2)
    near(1, K)
    wait(got.at[0, Q], got_sem.at[0, Q])
    near(1, V)
    near(1, Q)
    loop(turns, lambda turn: far_turn(0, turn))
    loop(turns, lambda turn: near_turn(0, turn))
    norm_keys(1)
    wait(got.at[1, V], got_sem.at[1, V])
    loop(turns, lambda turn: send_far(0, turn))
    wait(got.at[1, Q, pl.ds(0, half_rows)], got_sem.at[1, Q])
    loop(turns, lambda turn: near_turn(1, turn))

    def late_turn(turn):
        wait(got.at[1, Q, pl.ds(0, 2 * pair)], late_sem.at[turn])
        far_turn(1, turn)
        send_far(1, turn)

    loop(turns, late_turn)
    loop(turns, lambda turn: relay_turn(0, turn))
    loop(turns, lambda turn: relay_turn(1, turn))

    others = rows * (half_size - 1)
    for sample in range(samples):
        for part in range(3):
            wait(got.at[sample, part, pl.ds(0, others)], near_sent.at[sample, part])
    for slot in range(6):
        wait(by_row.at[0, pl.ds(0, others)], row_sent.at[slot])
        wait(by_row.at[0], half_sent.at[slot])
    wait(done.at[:, 0], out_sent.at[0])
    wait(got.at[0, pl.ds(0, 2), pl.ds(0, others)], out_sent.at[1])
    wait(got.at[0, pl.ds(0, 2), pl.ds(0, others)], relay_sent)
    wait(out, out_sem)

    @pl.when(replica == owner)
    def _():
        loop(replicas - 1, lambda step: wait(gains, gain_sent))


def shards(qkv, master, moment_one, moment_two, grads):
    updated, first_moment, second_moment = adamw(master, moment_one, moment_two, grads)
    layer = updated.astype(jnp.bfloat16)
    groups = lax.axis_size("seq")
    replicas = lax.axis_size("dp")
    _, _, samples, rows, width = qkv.shape
    patches = rows * groups
    attended = pl.pallas_call(
        functools.partial(kernel, groups, replicas),
        out_shape=jax.ShapeDtypeStruct((1, samples, rows, width), jnp.bfloat16),
        in_specs=[pl.BlockSpec(memory_space=pltpu.HBM), pl.BlockSpec(memory_space=pltpu.VMEM)],
        out_specs=pl.BlockSpec(memory_space=pl.ANY),
        scratch_shapes=[
            pltpu.VMEM(qkv.shape, jnp.bfloat16),
            pltpu.VMEM((samples, 3, patches, HD), jnp.bfloat16),
            pltpu.VMEM((3, patches // 2, HD), jnp.bfloat16),
            pltpu.VMEM((3, rows, groups // 2 * HD), jnp.bfloat16),
            pltpu.VMEM((samples, patches, HD), jnp.bfloat16),
            pltpu.VMEM((samples, 2, groups // 8, 4 * rows, HD), jnp.bfloat16),
            pltpu.VMEM((samples, groups // 8, 4 * rows, HD), jnp.bfloat16),
            pltpu.VMEM((4, HD), jnp.bfloat16),
            pltpu.SemaphoreType.DMA((samples, 3)),
            pltpu.SemaphoreType.DMA((samples, 3)),
            pltpu.SemaphoreType.DMA((groups // 8,)),
            pltpu.SemaphoreType.DMA((3,)),
            pltpu.SemaphoreType.DMA((3,)),
            pltpu.SemaphoreType.DMA((samples, groups // 8)),
            pltpu.SemaphoreType.DMA,
            pltpu.SemaphoreType.DMA,
            pltpu.SemaphoreType.DMA((samples, 3)),
            pltpu.SemaphoreType.DMA((6,)),
            pltpu.SemaphoreType.DMA((6,)),
            pltpu.SemaphoreType.DMA((2,)),
            pltpu.SemaphoreType.DMA,
            pltpu.SemaphoreType.DMA,
        ],
        compiler_params=pltpu.CompilerParams(
            collective_id=0, has_side_effects=True, vmem_limit_bytes=48 * 1024 * 1024
        ),
    )(pltpu.with_memory_space_constraint(qkv, pltpu.HBM), layer)
    return (attended, updated, first_moment, second_moment)


def solution(mesh):
    placed = (
        P(None, "dp", None, "seq", None),
        P(None, "dp"),
        P(None, "dp"),
        P(None, "dp"),
        P(None, "dp"),
    )
    return jax.shard_map(
        shards,
        mesh=mesh,
        in_specs=placed,
        out_specs=(P("dp", None, "seq", None), P(None, "dp"), P(None, "dp"), P(None, "dp")),
        check_vma=False,
    )
```

```python
import functools

import jax
import jax.numpy as jnp
from jax import lax
from jax.experimental import pallas as pl
from jax.experimental.pallas import tpu as pltpu
from jax.sharding import PartitionSpec as P

HEADS = 32
HD = 128
OPT_STEP = 10

BETA_ONE = 0.9
BETA_TWO = 0.95
RATE = 0.02
DECAY = 0.1
EPSILON = 1e-08

BLOCK = 256
SCORE_SCALE = HD**-0.5 * 1.4426950408889634
MESH = pl.DeviceIdType.MESH


def adamw(master, moment_one, moment_two, grads):
    first_moment = BETA_ONE * moment_one + (1.0 - BETA_ONE) * grads
    second_moment = BETA_TWO * moment_two + (1.0 - BETA_TWO) * grads * grads
    first_hat = first_moment / (1.0 - BETA_ONE**OPT_STEP)
    second_hat = second_moment / (1.0 - BETA_TWO**OPT_STEP)
    updated = master - RATE * (first_hat / (jnp.sqrt(second_hat) + EPSILON) + DECAY * master)
    return (updated, first_moment, second_moment)


def normalize(values, gain, bias):
    values = values.astype(jnp.float32)
    centred = values - jnp.mean(values, axis=-1, keepdims=True)
    spread = jnp.mean(centred * centred, axis=-1, keepdims=True)
    return (centred / jnp.sqrt(spread + 1e-06) * gain + bias).astype(jnp.bfloat16)


def attend(queries, keys, values):
    scores = lax.dot_general(
        queries, keys, (((1,), (1,)), ((), ())), preferred_element_type=jnp.float32
    )
    top = jnp.max(scores, axis=-1, keepdims=True)
    weights = jnp.exp2((scores - top) * SCORE_SCALE)
    total = jnp.sum(weights, axis=-1, keepdims=True)
    probs = (weights * (1.0 / total)).astype(jnp.bfloat16)
    out = jnp.dot(probs, values, preferred_element_type=jnp.float32)
    return out.astype(jnp.bfloat16)


def loop(count, body):
    def step(index, carry):
        body(index)
        return carry

    lax.fori_loop(0, count, step, 0)


def kernel(groups, replicas, stored, layer, out, qkv, got, by_row, by_half, keys, done, relay, gains,
           load_sem, got_sem, late_sem, row_sem, half_sem, relay_sem, out_sem, gain_sem,
           near_sent, row_sent, half_sent, out_sent, relay_sent, gain_sent):
    samples, rows = stored.shape[2], stored.shape[3]
    half_size = groups // 2
    chips = half_size // 2
    half_rows = rows * half_size
    me = lax.axis_index("seq")
    replica = lax.axis_index("dp")
    half, place = me // half_size, me % half_size
    chip, core = place // 2, place % 2
    opposite = (me + half_size) % groups
    owner = me * HD // layer.shape[1]

    def hops(turn):
        return (chips + chips // 2 + (turn + 1) // 2 * (1 - 2 * (turn % 2))) % chips

    def peer(step):
        return (chip + hops(step // 2)) % chips * 2 + (core + 1 - step % 2) % 2

    def at_rows(device):
        return pl.ds(pl.multiple_of(device * rows, rows), rows)

    def columns(device, count=1):
        return pl.ds(pl.multiple_of(device * HD, HD), count * HD)

    def push(source, target, sent, arrived, device):
        pltpu.make_async_remote_copy(
            source, target, sent, arrived, device_id=(replica, device), device_id_type=MESH
        ).start()

    def keep(source, target, arrived):
        pltpu.make_async_copy(source, target, arrived).start()

    def wait(ref, semaphore):
        pltpu.make_async_copy(ref, ref, semaphore).wait()

    Q, K, V = 0, 1, 2
    pair = 2 * rows
    turns = chips // 2

    def spots(turn):
        distance = turns - turn
        return (chip + distance) % chips, (chip + chips - distance % turns) % chips

    def chip_rows(which, seat):
        return pl.ds(pl.multiple_of(which * half_rows + seat * pair, pair), pair)

    for sample, part in ((0, K), (1, K), (0, V), (0, Q), (1, V), (1, Q)):
        keep(stored.at[part, 0, sample], qkv.at[part, 0, sample], load_sem.at[sample, part])

    def loaded(sample, part):
        wait(qkv.at[part, 0, sample], load_sem.at[sample, part])

    barrier = pltpu.get_barrier_semaphore()

    def greet_row(step, carry):
        device = half * half_size + peer(step)
        pl.semaphore_signal(barrier, 1, device_id=(replica, device), device_id_type=MESH)
        return carry

    def greet_dp(step, carry):
        other = (replica + step) % replicas
        pl.semaphore_signal(barrier, 1, device_id=(other, me), device_id_type=MESH)
        return carry

    pl.semaphore_signal(barrier, 1, device_id=(replica, opposite), device_id_type=MESH)
    lax.fori_loop(0, half_size - 1, greet_row, 0)
    lax.fori_loop(1, replicas, greet_dp, 0)
    pl.semaphore_wait(barrier, half_size - 1 + 1 + replicas - 1)

    own_layer = layer.at[:, pl.ds(pl.multiple_of(me * HD % layer.shape[1], HD), HD)]

    def near(sample, part):
        target = got.at[sample, part, at_rows(me), :]
        arrived = got_sem.at[sample, part]

        def send(step, carry):
            device = half * half_size + peer(step)
            source = qkv.at[part, 0, sample, :, columns(device)]
            push(source, target, near_sent.at[sample, part], arrived, device)
            return carry

        lax.fori_loop(0, half_size - 1, send, 0)
        keep(qkv.at[part, 0, sample, :, columns(me)], target, arrived)

    def row_first(sample, part, slot):
        target = by_row.at[slot, at_rows(place), :]

        def send(step, carry):
            seat = peer(step)
            source = qkv.at[part, 0, sample, :, columns((1 - half) * half_size + seat)]
            push(source, target, row_sent.at[slot], row_sem.at[slot], half * half_size + seat)
            return carry

        lax.fori_loop(0, half_size - 1, send, 0)
        source = qkv.at[part, 0, sample, :, columns(opposite)]
        keep(source, target, row_sem.at[slot])

    def row_then_half(sample, part, slot):
        wait(by_row.at[slot], row_sem.at[slot])
        at = pl.ds(pl.multiple_of(half * half_rows, half_rows), half_rows)
        push(
            by_row.at[slot], got.at[sample, part, at, :], half_sent.at[slot],
            got_sem.at[sample, part], opposite,
        )

    def row_then_half_by_turn(sample, part, slot):
        wait(by_row.at[slot], row_sem.at[slot])

        def send(turn):
            for seat in spots(turn):
                source = by_row.at[slot, pl.ds(pl.multiple_of(seat * pair, pair), pair), :]
                target = got.at[sample, part, chip_rows(half, seat), :]
                push(source, target, half_sent.at[slot], late_sem.at[turn], opposite)

        loop(turns, send)

    def half_first(sample, part, slot):
        source = qkv.at[part, 0, sample, :, columns((1 - half) * half_size, half_size)]
        push(source, by_half.at[slot], half_sent.at[3 + slot], half_sem.at[slot], opposite)

    def half_then_row(sample, part, slot):
        target = got.at[sample, part, at_rows(opposite), :]
        arrived = got_sem.at[sample, part]

        def send(step, carry):
            seat = peer(step)
            source = by_half.at[slot, :, columns(seat)]
            push(source, target, row_sent.at[3 + slot], arrived, half * half_size + seat)
            return carry

        lax.fori_loop(0, half_size - 1, send, 0)
        keep(by_half.at[slot, :, columns(place)], target, arrived)

    def norm_keys(sample):
        wait(got.at[sample, K], got_sem.at[sample, K])

        def norm_rows(step):
            at = pl.ds(pl.multiple_of(step * BLOCK, BLOCK), BLOCK)
            keys[sample, at, :] = normalize(got[sample, K, at, :], table[2:3], table[3:4])

        loop(keys.shape[1] // BLOCK, norm_rows)

    def attend_turn(sample, turn, which):
        ats = [chip_rows(which, seat) for seat in spots(turn)]
        block = jnp.concatenate([got[sample, Q, at, :] for at in ats], axis=0)
        queries = normalize(block, table[0:1], table[1:2])
        return attend(queries, keys[sample], got[sample, V])

    def far_turn(sample, turn):
        done[sample, 0, turn] = attend_turn(sample, turn, 1 - half)

    def send_far(sample, turn):
        push(
            done.at[sample, 0, turn], relay.at[sample, turn], out_sent.at[0],
            relay_sem.at[sample, turn], opposite,
        )

    def hand_out(source, head, sample, turn, sent):
        target = out.at[0, sample, :, columns(head)]
        for side, seat in enumerate(spots(turn)):
            for unit in range(2):
                piece = source.at[pl.ds(side * pair + unit * rows, rows), :]
                device = half * half_size + seat * 2 + unit

                @pl.when(device != me)
                def _():
                    push(piece, target, sent, out_sem, device)

                @pl.when(device == me)
                def _():
                    keep(piece, target, out_sem)

    def near_turn(sample, turn):
        done[sample, 1, turn] = attend_turn(sample, turn, half)
        hand_out(done.at[sample, 1, turn], me, sample, turn, out_sent.at[1])

    def relay_turn(sample, turn):
        wait(relay.at[sample, turn], relay_sem.at[sample, turn])
        hand_out(relay.at[sample, turn], opposite, sample, turn, relay_sent)

    loaded(0, K)
    half_first(0, K, 0)
    loaded(1, K)
    row_first(1, K, 0)
    loaded(0, V)
    half_first(0, V, 1)
    near(0, K)
    near(0, V)
    loaded(0, Q)
    near(0, Q)

    @pl.when(replica == owner)
    def _():
        def give(step, carry):
            pltpu.make_async_remote_copy(
                own_layer,
                gains,
                gain_sent,
                gain_sem,
                device_id=((replica + step) % replicas, me),
                device_id_type=MESH,
            ).start()
            return carry

        lax.fori_loop(1, replicas, give, 0)
        keep(own_layer, gains, gain_sem)

    wait(by_half.at[0], half_sem.at[0])
    half_first(0, Q, 2)
    half_then_row(0, K, 0)
    wait(by_half.at[1], half_sem.at[1])
    row_then_half(1, K, 0)
    half_then_row(0, V, 1)
    loaded(1, V)
    row_first(1, V, 1)
    wait(by_half.at[2], half_sem.at[2])
    row_then_half(1, V, 1)
    half_then_row(0, Q, 2)
    loaded(1, Q)
    row_first(1, Q, 2)

    wait(gains, gain_sem)
    table = gains[...].astype(jnp.float32)
    norm_keys(0)
    wait(got.at[0, V], got_sem.at[0, V])
    row_then_half_by_turn(1, Q, 2)
    near(1, K)
    wait(got.at[0, Q], got_sem.at[0, Q])
    near(1, V)
    near(1, Q)
    loop(turns, lambda turn: far_turn(0, turn))
    loop(turns, lambda turn: near_turn(0, turn))
    norm_keys(1)
    loop(turns, lambda turn: send_far(0, turn))
    wait(got.at[1, V], got_sem.at[1, V])
    wait(got.at[1, Q, pl.ds(0, half_rows)], got_sem.at[1, Q])
    loop(turns, lambda turn: near_turn(1, turn))

    def late_turn(turn):
        wait(got.at[1, Q, pl.ds(0, 2 * pair)], late_sem.at[turn])
        far_turn(1, turn)
        send_far(1, turn)

    loop(turns, late_turn)
    loop(turns, lambda turn: relay_turn(0, turn))
    loop(turns, lambda turn: relay_turn(1, turn))

    others = rows * (half_size - 1)
    for sample in range(samples):
        for part in range(3):
            wait(got.at[sample, part, pl.ds(0, others)], near_sent.at[sample, part])
    for slot in range(6):
        wait(by_row.at[0, pl.ds(0, others)], row_sent.at[slot])
        wait(by_row.at[0], half_sent.at[slot])
    wait(done.at[:, 0], out_sent.at[0])
    wait(got.at[0, pl.ds(0, 2), pl.ds(0, others)], out_sent.at[1])
    wait(got.at[0, pl.ds(0, 2), pl.ds(0, others)], relay_sent)
    wait(out, out_sem)

    @pl.when(replica == owner)
    def _():
        loop(replicas - 1, lambda step: wait(gains, gain_sent))


def shards(qkv, master, moment_one, moment_two, grads):
    updated, first_moment, second_moment = adamw(master, moment_one, moment_two, grads)
    layer = updated.astype(jnp.bfloat16)
    groups = lax.axis_size("seq")
    replicas = lax.axis_size("dp")
    _, _, samples, rows, width = qkv.shape
    patches = rows * groups
    attended = pl.pallas_call(
        functools.partial(kernel, groups, replicas),
        out_shape=jax.ShapeDtypeStruct((1, samples, rows, width), jnp.bfloat16),
        in_specs=[pl.BlockSpec(memory_space=pltpu.HBM), pl.BlockSpec(memory_space=pltpu.VMEM)],
        out_specs=pl.BlockSpec(memory_space=pl.ANY),
        scratch_shapes=[
            pltpu.VMEM(qkv.shape, jnp.bfloat16),
            pltpu.VMEM((samples, 3, patches, HD), jnp.bfloat16),
            pltpu.VMEM((3, patches // 2, HD), jnp.bfloat16),
            pltpu.VMEM((3, rows, groups // 2 * HD), jnp.bfloat16),
            pltpu.VMEM((samples, patches, HD), jnp.bfloat16),
            pltpu.VMEM((samples, 2, groups // 8, 4 * rows, HD), jnp.bfloat16),
            pltpu.VMEM((samples, groups // 8, 4 * rows, HD), jnp.bfloat16),
            pltpu.VMEM((4, HD), jnp.bfloat16),
            pltpu.SemaphoreType.DMA((samples, 3)),
            pltpu.SemaphoreType.DMA((samples, 3)),
            pltpu.SemaphoreType.DMA((groups // 8,)),
            pltpu.SemaphoreType.DMA((3,)),
            pltpu.SemaphoreType.DMA((3,)),
            pltpu.SemaphoreType.DMA((samples, groups // 8)),
            pltpu.SemaphoreType.DMA,
            pltpu.SemaphoreType.DMA,
            pltpu.SemaphoreType.DMA((samples, 3)),
            pltpu.SemaphoreType.DMA((6,)),
            pltpu.SemaphoreType.DMA((6,)),
            pltpu.SemaphoreType.DMA((2,)),
            pltpu.SemaphoreType.DMA,
            pltpu.SemaphoreType.DMA,
        ],
        compiler_params=pltpu.CompilerParams(
            collective_id=0, has_side_effects=True, vmem_limit_bytes=48 * 1024 * 1024
        ),
    )(pltpu.with_memory_space_constraint(qkv, pltpu.HBM), layer)
    return (attended, updated, first_moment, second_moment)


def solution(mesh):
    placed = (
        P(None, "dp", None, "seq", None),
        P(None, "dp"),
        P(None, "dp"),
        P(None, "dp"),
        P(None, "dp"),
    )
    return jax.shard_map(
        shards,
        mesh=mesh,
        in_specs=placed,
        out_specs=(P("dp", None, "seq", None), P(None, "dp"), P(None, "dp"), P(None, "dp")),
        check_vma=False,
    )
```
